32 devices in a mesh: region: 4 (over y, x), worker: 8 (over z, core).
Axes of the slice: x: 2, y: 2, z: 4, core: 2. Of those that a mesh axis runs over, the one named last changes fastest.
Arguments:
- worker_start: bfloat16 [4, 128, 4096], P('region'), may hold values from -0.5 to 0.5
- inputs: bfloat16 [4, 8, 4, 256, 128], P('region', 'worker'), may hold values from -6 to 6
- teacher: bfloat16 [128, 4096], replicated, may hold values from -0.5 to 0.5
- regional_momentum: float32 [4, 128, 4096], P('region', 'worker'), may hold values from -1.5 to 1.5
- global_params: float32 [128, 4096], P('worker', 'region'), may hold values from -6 to 6
- global_momentum: float32 [128, 4096], P('worker', 'region'), may hold values from -1.5 to 1.5
- staleness: int32 [4], replicated, may hold values from 0 to 4
- arrival_order: int32 [4], replicated, may hold values from 0 to 3, as said below
- pull_slot: int32 [4], replicated, may hold values from 0 to 3, as said below
Outputs:
- momentum_regional: float32 [4, 128, 4096], P('region', 'worker')
- params_global: float32 [128, 4096], P('worker', 'region')
- momentum_global: float32 [128, 4096], P('worker', 'region')
- worker_params: float32 [4, 128, 4096], P('region')
The draws below stay inside these ranges and needn't reach their ends.
Inputs may be any that keep to these rules, and one draw needn't show every extreme that they name: arrival_order is a permutation of the regions 0 .. 3. pull_slot[r] is at least the position of region r in arrival_order; the region that arrives first has slot 0.
All inputs are finite; a program needn't handle non-finite values.
Results may differ from the reference program's by a relative error of at most 0.00043.
Values sent between devices are 32-bit elements; how exact they have to be, the bound alone decides.
No kernel may reach another device: no remote copies, remote signals or barrier semaphores. Data moves between devices by JAX's collectives and lax.ppermute only.
A program may use at most 64 MiB of HBM per device.

```python
import jax
import jax.numpy as jnp
from jax import lax

D = 4096
ROWS = 128
TOK = 256
STEPS = 4
REGIONS = 4
WORKERS = 8


def arrival_plan(key):
    arrival = jax.random.permutation(jax.random.fold_in(key, 31), REGIONS).astype(jnp.int32)
    position = jnp.argsort(arrival).astype(jnp.int32)
    extra = jax.random.randint(jax.random.fold_in(key, 37), (REGIONS,), 0, REGIONS - position).astype(jnp.int32)
    slots = jnp.where(position == 0, 0, position + extra).astype(jnp.int32)
    return (arrival, slots)


def draw_arrival_order(key, part):
    return arrival_plan(key)[0]


def draw_pull_slot(key, part):
    return arrival_plan(key)[1]


def set_ends(result, key, least, high):
    longest = result.shape.index(max(result.shape))
    spots = []
    for shift in (0, 1):
        where = [jax.random.randint(jax.random.fold_in(key, axis), (), 0, length) for axis, length in enumerate(result.shape)]
        where[longest] = (where[longest] + shift) % result.shape[longest]
        spots.append(tuple(where))
    return result.at[spots[0]].set(least).at[spots[1]].set(high)


def block_scale(rng, dims, shards, least, top_value):
    loudness, own = 1.0, jax.random.fold_in(rng, 6)
    for axis_at, shards_of in shards:
        draws = jnp.exp(jax.random.uniform(jax.random.fold_in(own, axis_at), (shards_of,), jnp.float32, least / len(shards), top_value / len(shards)))
        loudness = loudness * jnp.repeat(draws, dims[axis_at] // shards_of).reshape([-1 if axis == axis_at else 1 for axis in range(len(dims))])
    return loudness


def gaussian(rng, extent, deviation, reach, shards=(), held_as=jnp.bfloat16):
    level = block_scale(rng, extent, shards, -0.22, 0.18) if shards else 1.0
    drawn = jax.random.normal(rng, extent, jnp.float32) * deviation * level
    return jnp.minimum(jnp.maximum(drawn, -reach), reach).astype(held_as)


def setup_inputs(seed: int = 0) -> dict:
    arg_keys = jax.random.split(jax.random.key(seed), 10)
    return {
        "worker_start": gaussian(arg_keys[0], (REGIONS, ROWS, D), ROWS ** -0.5, 0.5, ((0, 4),)),
        "inputs": gaussian(arg_keys[1], (REGIONS, WORKERS, STEPS, TOK, ROWS), 1.0, 6.0, ((0, 4), (1, 8))),
        "teacher": gaussian(arg_keys[2], (ROWS, D), ROWS ** -0.5, 0.5),
        "regional_momentum": gaussian(arg_keys[3], (REGIONS, ROWS, D), 0.1, 1.5, ((0, 4), (1, 8)), jnp.float32),
        "global_params": gaussian(arg_keys[4], (ROWS, D), 0.5, 6.0, ((0, 8), (1, 4)), jnp.float32),
        "global_momentum": gaussian(arg_keys[5], (ROWS, D), 0.1, 1.5, ((0, 8), (1, 4)), jnp.float32),
        "staleness": set_ends(jax.random.randint(arg_keys[6], (REGIONS,), 0, 5), jax.random.fold_in(arg_keys[6], 1), 0, 4).astype(jnp.int32),
        "arrival_order": draw_arrival_order(jax.random.fold_in(arg_keys[9], 71), 0),
        "pull_slot": draw_pull_slot(jax.random.fold_in(arg_keys[9], 71), 0),
    }


LOCAL_RATE = 0.3
REGION_BETA = 0.9
REGION_RATE = 1.0
GLOBAL_MU = 0.9
GLOBAL_RATE = 0.7


def residual_of(weights, micro_batch, teacher):
    target = jax.nn.silu(jnp.dot(micro_batch, teacher, preferred_element_type=jnp.float32))
    predicted = jnp.dot(micro_batch, weights.astype(jnp.bfloat16), preferred_element_type=jnp.float32)
    return (predicted - target).astype(jnp.bfloat16)


def gradient_of(micro_batch, residual):
    return lax.dot_general(micro_batch, residual, (((0,), (0,)), ((), ())), preferred_element_type=jnp.float32)


def pseudo_gradient(initial, hidden, teacher):
    start_weights = initial.astype(jnp.float32)
    step_scale = LOCAL_RATE / hidden.shape[1]
    current = start_weights
    for local_step in range(hidden.shape[0]):
        residual = residual_of(current, hidden[local_step], teacher)
        current = current - step_scale * gradient_of(hidden[local_step], residual)
    return start_weights - current


def reference(worker_start, inputs, teacher, regional_momentum, global_params, global_momentum, staleness, arrival_order, pull_slot):
    def one_region(region_args):
        initial, region_inputs, momentum = region_args

        def add_worker(total, worker_inputs):
            pseudo = pseudo_gradient(initial, worker_inputs, teacher)
            return total + pseudo, None

        summed, unused = lax.scan(add_worker, jnp.zeros(initial.shape, jnp.float32), region_inputs)
        momentum_new = REGION_BETA * momentum + summed / WORKERS
        return momentum_new, REGION_RATE * momentum_new

    momentum_regional, deltas = lax.map(one_region, (worker_start, inputs, regional_momentum))
    weights = 1.0 / (1.0 + staleness.astype(jnp.float32))

    def advance(state_pair, arrival):
        params_now, momentum_now = state_pair
        source = arrival_order[arrival]
        update = weights[source] * deltas[source]
        momentum_now = GLOBAL_MU * momentum_now + update
        params_now = params_now - GLOBAL_RATE * (update + GLOBAL_MU * momentum_now)
        return (params_now, momentum_now), params_now

    (params_global, momentum_global), versions = lax.scan(advance, (global_params, global_momentum), jnp.arange(REGIONS, dtype=jnp.int32))
    pulled = versions[pull_slot]
    return momentum_regional, params_global, momentum_global, pulled
```

```python
import functools

import jax
import jax.numpy as jnp
from jax import lax
from jax.experimental import pallas as pl
from jax.experimental.pallas import tpu as pltpu
from jax.sharding import PartitionSpec as P

LOCAL_RATE = 0.3
REGION_BETA = 0.9
REGION_RATE = 1.0
GLOBAL_MU = 0.9
GLOBAL_RATE = 0.7

CHUNKS = 4
F32 = jnp.float32
BF16 = jnp.bfloat16
VMEM = pl.BlockSpec(memory_space=pltpu.VMEM)
SMEM = pl.BlockSpec(memory_space=pltpu.SMEM)
ANY = pl.BlockSpec(memory_space=pl.ANY)


def call(kernel, out, in_specs, out_specs, cost, name, **kwargs):
    flops, moved = cost
    return pl.pallas_call(
        kernel,
        out_shape=out,
        in_specs=in_specs,
        out_specs=out_specs,
        cost_estimate=pl.CostEstimate(flops=flops, bytes_accessed=moved, transcendentals=0),
        compiler_params=pltpu.CompilerParams(vmem_limit_bytes=16 * 1024 * 1024),
        name=name,
        **kwargs,
    )


def steps_kernel(offset, stride, pos_ref, x_ref, w_ref, t_ref, keep_ref, send_ref):
    core, chip = pos_ref[0], pos_ref[1]
    chips, strips, rows, width = keep_ref.shape
    local_steps, tokens, _ = x_ref.shape
    scale = LOCAL_RATE / tokens

    def columns(ref):
        return jnp.concatenate(
            [ref[:, s * stride + offset : s * stride + offset + width] for s in range(strips)], 1
        )

    start = columns(w_ref).astype(F32)
    half_teacher = (columns(t_ref).astype(F32) * 0.5).astype(BF16)

    def target(step):
        half = jnp.dot(x_ref[step], half_teacher, preferred_element_type=F32)
        return half + half * jnp.tanh(half)

    current = start
    wanted = target(0)
    for step in range(local_steps):
        x = x_ref[step]
        predicted = jnp.dot(x, current.astype(BF16), preferred_element_type=F32)
        residual = (predicted - wanted).astype(BF16)
        if step + 1 < local_steps:
            wanted = target(step + 1)
        gradient = lax.dot_general(
            x, residual, (((0,), (0,)), ((), ())), preferred_element_type=F32
        )
        current = current - scale * gradient
    pseudo = start - current
    for k in range(chips):
        slot = k ^ chip
        for s in range(strips):
            even = pseudo[2 * k * rows : (2 * k + 1) * rows, s * width : (s + 1) * width]
            odd = pseudo[(2 * k + 1) * rows : (2 * k + 2) * rows, s * width : (s + 1) * width]
            keep_ref[slot, s] = jnp.where(core == 0, even, odd)
            send_ref[slot, s] = jnp.where(core == 0, odd, even)


def add_kernel(keep_ref, got_ref, *out_refs):
    for k, out in enumerate(out_refs):
        out[...] = keep_ref[k] + got_ref[k]


def momentum_kernel(offset, stride, workers, *refs):
    *parts, old_ref, out_ref = refs
    strips, _, width = out_ref.shape
    for s in range(strips):
        total = parts[0][s]
        for part in parts[1:]:
            total = total + part[s]
        first = s * stride + offset
        out_ref[s] = REGION_RATE * (
            REGION_BETA * old_ref[:, first : first + width] + total / workers
        )


def merge_kernel(offset, regions, pos_ref, coef_ref, *refs):
    deltas, states = refs[:regions], refs[regions : 2 * regions]
    pulled_ref, params_ref, momentum_ref = refs[2 * regions :]
    me = pos_ref[2]
    width = pulled_ref.shape[2]
    for q in range(regions):
        strip = me ^ q
        params = states[q][0, :, offset : offset + width]
        momentum = states[q][1, :, offset : offset + width]
        terms = [deltas[p][strip] for p in range(regions)]
        pulled = params - coef_ref[0, regions] * momentum
        for p in range(regions):
            pulled = pulled - coef_ref[0, p] * terms[p]
        pulled_ref[strip] = pulled
        if q == 0:
            last = params - coef_ref[1, regions] * momentum
            carried = coef_ref[2, regions] * momentum
            for p in range(regions):
                last = last - coef_ref[1, p] * terms[p]
                carried = carried + coef_ref[2, p] * terms[p]
            params_ref[...] = last
            momentum_ref[...] = carried


def place_kernel(offset, stride, blocks, aliased, *refs):
    pos_ref, *rest = refs
    parts = rest[: blocks + 3]
    outs = rest[blocks + 3 + aliased : -1]
    sems = rest[-1]
    core, chip = pos_ref[0], pos_ref[1]
    pulled_ref, regional_ref, params_ref, momentum_ref = outs
    strips, _, width = parts[0].shape
    copies = []

    def copy(source, target):
        copies.append(pltpu.make_async_copy(source, target, sems.at[len(copies)]))
        copies[-1].start()

    for s in range(strips):
        columns = pl.ds(s * stride + offset, width)
        for b in range(blocks):
            owner = 2 * (chip ^ (b // 2)) + (core ^ (b % 2))
            copy(parts[b].at[s], pulled_ref.at[owner, :, columns])
        copy(parts[blocks].at[s], regional_ref.at[:, columns])
    copy(parts[blocks + 1], params_ref.at[:, pl.ds(offset, width)])
    copy(parts[blocks + 2], momentum_ref.at[:, pl.ds(offset, width)])
    for one in copies:
        one.wait()


def exchange(value, axis, bits):
    size = lax.axis_size(axis)
    return lax.ppermute(value, axis, [(i, i ^ bits) for i in range(size)])


def scatter_sum(blocks):
    bit, count = 1, len(blocks)
    while count > 4:
        got = exchange(jnp.stack(blocks[1::2]), "worker", 2 * bit)
        blocks = [b + got[i] for i, b in enumerate(blocks[0::2])]
        bit, count = 2 * bit, count // 2
    if count == 4:
        far = exchange(blocks[3], "worker", 2 * bit)
        near = exchange(blocks[1], "worker", 2 * bit)
        across = exchange(blocks[2] + far, "worker", 4 * bit)
        return [blocks[0], near, across]
    if count == 2:
        return [blocks[0], exchange(blocks[1], "worker", 2 * bit)]
    return blocks


def gather_blocks(block, chips):
    levels = chips.bit_length() - 1
    if levels >= 2:
        bit = chips // 4
        near = exchange(block, "worker", 2 * bit)
        across = exchange(block, "worker", 4 * bit)
        far = exchange(across, "worker", 2 * bit)
        blocks, bit = [block, near, across, far], bit // 2
    elif levels == 1:
        blocks, bit = [block, exchange(block, "worker", 2)], 0
    else:
        blocks, bit = [block], 0
    while bit >= 1:
        got = exchange(jnp.stack(blocks), "worker", 2 * bit)
        blocks = [part for i, b in enumerate(blocks) for part in (b, got[i])]
        bit //= 2
    return [part for b in blocks for part in (b, exchange(b, "worker", 1))]


def coefficients(staleness, arrival_order, pull_slot, region):
    count = arrival_order.shape[0]
    seen = jnp.arange(count, dtype=jnp.int32)
    relative = region ^ seen
    hits = arrival_order[None, :] == relative[:, None]
    position = jnp.sum(jnp.where(hits, seen[None, :], 0), axis=1)
    here = relative[:, None] == seen[None, :]
    stale = jnp.sum(jnp.where(here, staleness[None, :], 0), axis=1)
    slot = jnp.sum(jnp.where(seen == region, pull_slot, 0))
    weight = 1.0 / (1.0 + stale.astype(F32))
    step, own, carried = [], [], []
    total, power = 1.0, 1.0
    for _ in range(count):
        carried.append(power)
        power *= GLOBAL_MU
        total += power
        step.append(GLOBAL_RATE * total)
        own.append(GLOBAL_RATE * GLOBAL_MU * (total - 1.0))

    def pick(table, index):
        hit = index[..., None] == seen
        return jnp.sum(jnp.where(hit, jnp.array(table, F32), 0.0), axis=-1)

    last = count - 1
    deltas = jnp.stack(
        [pick(step, slot - position), pick(step, last - position), pick(carried, last - position)]
    )
    olds = jnp.stack([pick(own, slot), jnp.array(own[last], F32), jnp.array(power, F32)])
    return jnp.concatenate([deltas * weight[None, :], olds[:, None]], axis=1)


def local(
    worker_start,
    inputs,
    teacher,
    regional_momentum,
    global_params,
    global_momentum,
    staleness,
    arrival_order,
    pull_slot,
):
    initial, hidden, old = worker_start[0], inputs[0, 0], regional_momentum[0]
    depth, wide = initial.shape
    workers, regions = lax.axis_size("worker"), lax.axis_size("region")
    chips, rows, stride = workers // 2, depth // workers, wide // regions
    chunks = min(CHUNKS, stride // 128)
    width = stride // chunks
    region, worker = lax.axis_index("region"), lax.axis_index("worker")
    pos = jnp.stack([worker % 2, worker // 2, region]).astype(jnp.int32)
    coef = coefficients(staleness, arrival_order, pull_slot, region)
    state = jnp.stack([global_params, global_momentum])
    states = [state] + [exchange(state, "region", q) for q in range(1, regions)]

    block = jax.ShapeDtypeStruct((regions, rows, width), F32)
    strip = jax.ShapeDtypeStruct((rows, width), F32)
    half = jax.ShapeDtypeStruct((chips, regions, rows, width), F32)
    block_bytes = regions * rows * width * 4
    outs = None
    for j in range(chunks):
        offset = j * width
        keep, send = call(
            functools.partial(steps_kernel, offset, stride),
            (half, half),
            [SMEM, VMEM, VMEM, VMEM],
            (VMEM, VMEM),
            (6 * hidden.shape[0] * hidden.shape[1] * depth * width * regions, 2 * workers * block_bytes),
            f"steps_{j}",
        )(pos, hidden, initial, teacher)
        got = exchange(send, "worker", 1)
        blocks = call(
            add_kernel, (block,) * chips, [VMEM] * 2, (VMEM,) * chips,
            (0, 3 * chips * block_bytes), f"add_{j}",
        )(keep, got)
        parts = scatter_sum(blocks)
        delta = call(
            functools.partial(momentum_kernel, offset, stride, workers),
            block, [VMEM] * (len(parts) + 1), VMEM,
            (0, (len(parts) + 2) * block_bytes), f"momentum_{j}",
        )(*parts, old)
        deltas = [delta] + [exchange(delta, "region", q) for q in range(1, regions)]
        pulled, last, carried = call(
            functools.partial(merge_kernel, offset, regions),
            (block, strip, strip),
            [SMEM, SMEM] + [VMEM] * (2 * regions),
            (VMEM,) * 3,
            (0, (regions + 4) * block_bytes), f"merge_{j}",
        )(pos, coef, *deltas, *states)
        pieces = gather_blocks(pulled, chips) + [delta, last, carried]
        shapes = (
            jax.ShapeDtypeStruct((workers, rows, wide), F32),
            jax.ShapeDtypeStruct((rows, wide), F32),
            jax.ShapeDtypeStruct((rows, stride), F32),
            jax.ShapeDtypeStruct((rows, stride), F32),
        )
        before = () if outs is None else outs
        outs = call(
            functools.partial(place_kernel, offset, stride, workers, len(before)),
            shapes,
            [SMEM] + [VMEM] * len(pieces) + [ANY] * len(before),
            (ANY,) * 4,
            (0, 2 * workers * block_bytes), f"place_{j}",
            scratch_shapes=[pltpu.SemaphoreType.DMA((regions * (workers + 1) + 2,))],
            input_output_aliases={1 + len(pieces) + i: i for i in range(len(before))},
        )(pos, *pieces, *before)
    pulled, regional, params, momentum = outs
    return (regional[None], params, momentum, pulled.reshape(depth, wide)[None])


def solution(mesh):
    placed = (
        P("region", None, None),
        P("region", "worker", None, None, None),
        P(),
        P("region", "worker", None),
        P("worker", "region"),
        P("worker", "region"),
        P(),
        P(),
        P(),
    )
    return jax.shard_map(
        local,
        mesh=mesh,
        in_specs=placed,
        out_specs=(
            P("region", "worker", None),
            P("worker", "region"),
            P("worker", "region"),
            P("region", None, None),
        ),
        check_vma=False,
    )
```

```python
import functools

import jax
import jax.numpy as jnp
from jax import lax
from jax.experimental import pallas as pl
from jax.experimental.pallas import tpu as pltpu
from jax.sharding import PartitionSpec as P

LOCAL_RATE = 0.3
REGION_BETA = 0.9
REGION_RATE = 1.0
GLOBAL_MU = 0.9
GLOBAL_RATE = 0.7

CHUNKS = 2
F32 = jnp.float32
BF16 = jnp.bfloat16
VMEM = pl.BlockSpec(memory_space=pltpu.VMEM)
SMEM = pl.BlockSpec(memory_space=pltpu.SMEM)
HBM = pl.BlockSpec(memory_space=pltpu.HBM)


def call(kernel, out, in_specs, out_specs, moved, flops=0, grant=20, **kwargs):
    return pl.pallas_call(
        kernel,
        out_shape=out,
        in_specs=in_specs,
        out_specs=out_specs,
        cost_estimate=pl.CostEstimate(flops=flops, bytes_accessed=moved, transcendentals=0),
        compiler_params=pltpu.CompilerParams(vmem_limit_bytes=grant * 1024 * 1024),
        **kwargs,
    )


def exchange(value, axis, bits):
    size = lax.axis_size(axis)
    return lax.ppermute(value, axis, [(i, i ^ bits) for i in range(size)])


def place_of_mine():
    worker = lax.axis_index("worker")
    return lax.rem(worker, 2), lax.div(worker, 2)


def take_steps(x_ref, start, half_teacher, keep_ref, send_ref):
    core, chip = place_of_mine()
    chips, strips, rows, width = keep_ref.shape
    local_steps, tokens, _ = x_ref.shape
    scale = LOCAL_RATE / tokens

    def target(step):
        half = jnp.dot(x_ref[step], half_teacher, preferred_element_type=F32)
        return half + half * jnp.tanh(half)

    current = start
    wanted = target(0)
    for step in range(local_steps):
        x = x_ref[step]
        predicted = jnp.dot(x, current.astype(BF16), preferred_element_type=F32)
        residual = (predicted - wanted).astype(BF16)
        if step + 1 < local_steps:
            wanted = target(step + 1)
        gradient = lax.dot_general(
            x, residual, (((0,), (0,)), ((), ())), preferred_element_type=F32
        )
        current = current - scale * gradient
    pseudo = start - current
    for k in range(chips):
        slot = k ^ chip
        for s in range(strips):
            even = pseudo[2 * k * rows : (2 * k + 1) * rows, s * width : (s + 1) * width]
            odd = pseudo[(2 * k + 1) * rows : (2 * k + 2) * rows, s * width : (s + 1) * width]
            keep_ref[slot, s] = jnp.where(core == 0, even, odd)
            send_ref[slot, s] = jnp.where(core == 0, odd, even)


def halved(teacher):
    return (teacher.astype(F32) * 0.5).astype(BF16)


def first_kernel(stride, has_rest, x_hbm, w_hbm, t_hbm, keep_ref, send_ref, *refs):
    if has_rest:
        x_ref, w_rest, t_rest, w_ref, t_ref, sems = refs
    else:
        x_ref, w_ref, t_ref, sems = refs
    _, strips, _, width = keep_ref.shape
    now, later = [], []

    def copy(source, target, group):
        one = pltpu.make_async_copy(source, target, sems.at[len(now) + len(later)])
        one.start()
        group.append(one)

    copy(x_hbm, x_ref, now)
    for source, target in ((t_hbm, t_ref), (w_hbm, w_ref)):
        for s in range(strips):
            columns = pl.ds(s * width, width)
            copy(source.at[:, pl.ds(s * stride, width)], target.at[:, columns], now)
    if has_rest:
        for source, target in ((t_hbm, t_rest), (w_hbm, w_rest)):
            for s in range(strips):
                columns = pl.ds(s * stride + width, stride - width)
                copy(source.at[:, columns], target.at[s], later)
    for one in now:
        one.wait()
    take_steps(x_ref, w_ref[...].astype(F32), halved(t_ref[...]), keep_ref, send_ref)
    for one in later:
        one.wait()


def later_kernel(offset, x_ref, w_ref, t_ref, keep_ref, send_ref):
    _, strips, _, width = keep_ref.shape

    def columns(ref):
        return jnp.concatenate([ref[s, :, offset : offset + width] for s in range(strips)], 1)

    take_steps(x_ref, columns(w_ref).astype(F32), halved(columns(t_ref)), keep_ref, send_ref)


def add_kernel(keep_ref, got_ref, *out_refs):
    for k, out in enumerate(out_refs):
        out[...] = keep_ref[k] + got_ref[k]


def momentum_kernel(offset, stride, workers, *refs):
    *parts, old_ref, out_ref = refs
    strips, _, width = out_ref.shape
    for s in range(strips):
        total = parts[0][s]
        for part in parts[1:]:
            total = total + part[s]
        first = s * stride + offset
        out_ref[s] = REGION_RATE * (
            REGION_BETA * old_ref[:, first : first + width] + total / workers
        )


def coefficient_kernel(stale_ref, arrival_ref, slot_ref, coef_ref):
    _, regions, width = coef_ref.shape
    regions -= 1
    step, own, carried = [], [], []
    total, power = 1.0, 1.0
    for _ in range(regions):
        carried.append(power)
        power *= GLOBAL_MU
        total += power
        step.append(GLOBAL_RATE * total)
        own.append(GLOBAL_RATE * GLOBAL_MU * (total - 1.0))

    def pick(table, index):
        value = jnp.zeros((1, width), F32)
        for i, entry in enumerate(table):
            value = jnp.where(index == i, entry, value)
        return value

    region = lax.axis_index("region")
    slot, last = slot_ref[region], regions - 1
    for q in range(regions):
        other = region ^ q
        position = jnp.int32(0)
        for k in range(regions):
            position = jnp.where(arrival_ref[k] == other, k, position)
        weight = 1.0 / (1.0 + jnp.full((1, width), stale_ref[other], jnp.int32).astype(F32))
        coef_ref[0, q : q + 1] = weight * pick(step, slot - position)
        coef_ref[1, q : q + 1] = weight * pick(step, last - position)
        coef_ref[2, q : q + 1] = weight * pick(carried, last - position)
    coef_ref[0, regions : regions + 1] = pick(own, slot)
    coef_ref[1, regions : regions + 1] = jnp.full((1, width), own[last], F32)
    coef_ref[2, regions : regions + 1] = jnp.full((1, width), power, F32)


def merge_kernel(offset, regions, coef_ref, *refs):
    deltas, states = refs[:regions], refs[regions : 2 * regions]
    pulled_ref, params_ref, momentum_ref = refs[2 * regions :]
    me = lax.axis_index("region")
    width = pulled_ref.shape[2]

    def coef(row, column):
        return coef_ref[row, column : column + 1]

    for q in range(regions):
        strip = me ^ q
        params = states[q][0, :, offset : offset + width]
        momentum = states[q][1, :, offset : offset + width]
        terms = [deltas[p][strip] for p in range(regions)]
        pulled = params - coef(0, regions) * momentum
        for p in range(regions):
            pulled = pulled - coef(0, p) * terms[p]
        pulled_ref[strip] = pulled
        if q == 0:
            last = params - coef(1, regions) * momentum
            carried = coef(2, regions) * momentum
            for p in range(regions):
                last = last - coef(1, p) * terms[p]
                carried = carried + coef(2, p) * terms[p]
            params_ref[...] = last
            momentum_ref[...] = carried


def place_kernel(offset, stride, owners, side, aliased, *refs):
    count = len(owners) + (3 if side else 0)
    parts, outs, sems = refs[:count], refs[count + aliased : -1], refs[-1]
    core, chip = place_of_mine()
    strips, _, width = parts[0].shape
    copies = []

    def copy(source, target):
        copies.append(pltpu.make_async_copy(source, target, sems.at[len(copies)]))
        copies[-1].start()

    for s in range(strips):
        columns = pl.ds(s * stride + offset, width)
        for part, b in zip(parts, owners):
            owner = 2 * (chip ^ (b // 2)) + (core ^ (b % 2))
            copy(part.at[s], outs[0].at[owner, :, columns])
        if side:
            copy(parts[-3].at[s], outs[1].at[:, columns])
    if side:
        copy(parts[-2], outs[2].at[:, pl.ds(offset, width)])
        copy(parts[-1], outs[3].at[:, pl.ds(offset, width)])
    for one in copies:
        one.wait()


def scatter_sum(blocks):
    bit, count = 1, len(blocks)
    while count > 4:
        got = exchange(jnp.stack(blocks[1::2]), "worker", 2 * bit)
        blocks = [b + got[i] for i, b in enumerate(blocks[0::2])]
        bit, count = 2 * bit, count // 2
    if count == 4:
        far = exchange(blocks[3], "worker", 2 * bit)
        near = exchange(blocks[1], "worker", 2 * bit)
        across = exchange(blocks[2] + far, "worker", 4 * bit)
        return [blocks[0], near, across]
    if count == 2:
        return [blocks[0], exchange(blocks[1], "worker", 2 * bit)]
    return blocks


def gather_blocks(block, chips):
    levels = chips.bit_length() - 1
    if levels >= 2:
        bit = chips // 4
        across = exchange(block, "worker", 4 * bit)
        near = exchange(block, "worker", 2 * bit)
        far = exchange(across, "worker", 2 * bit)
        blocks, bit = [block, near, across, far], bit // 2
    elif levels == 1:
        blocks, bit = [block, exchange(block, "worker", 2)], 0
    else:
        blocks, bit = [block], 0
    while bit >= 1:
        got = exchange(jnp.stack(blocks), "worker", 2 * bit)
        blocks = [part for i, b in enumerate(blocks) for part in (b, got[i])]
        bit //= 2
    return [part for b in blocks for part in (b, exchange(b, "worker", 1))]


def local(
    worker_start,
    inputs,
    teacher,
    regional_momentum,
    global_params,
    global_momentum,
    staleness,
    arrival_order,
    pull_slot,
):
    initial, hidden, old = worker_start[0], inputs[0, 0], regional_momentum[0]
    depth, wide = initial.shape
    workers, regions = lax.axis_size("worker"), lax.axis_size("region")
    chips, rows, stride = workers // 2, depth // workers, wide // regions
    chunks = min(CHUNKS, stride // 128)
    width = stride // chunks

    def shape(*dims, dtype=F32):
        return jax.ShapeDtypeStruct(dims, dtype)

    coef = call(
        coefficient_kernel, shape(3, regions + 1, width), [SMEM] * 3, VMEM, 4096
    )(staleness, arrival_order, pull_slot)
    state = jnp.stack([global_params, global_momentum])
    states = [state] + [exchange(state, "region", q) for q in range(1, regions)]

    block = shape(regions, rows, width)
    half = shape(chips, regions, rows, width)
    block_bytes = regions * rows * width * 4
    flops = 6 * hidden.shape[0] * hidden.shape[1] * depth * width * regions
    has_rest = chunks > 1
    rest = (shape(regions, depth, stride - width, dtype=initial.dtype),) * 2 if has_rest else ()
    chunk_columns = pltpu.VMEM((depth, regions * width), initial.dtype)
    keep, send, x_ready, *ready = call(
        functools.partial(first_kernel, stride, has_rest),
        (half, half, shape(*hidden.shape, dtype=hidden.dtype), *rest),
        [HBM] * 3,
        (VMEM,) * (3 + len(rest)),
        2 * workers * block_bytes,
        flops,
        grant=51,
        scratch_shapes=[
            chunk_columns, chunk_columns, pltpu.SemaphoreType.DMA((1 + 4 * regions,))
        ],
    )(hidden, initial, teacher)
    halves = [(keep, send)]
    for j in range(1, chunks):
        halves.append(
            call(
                functools.partial(later_kernel, (j - 1) * width),
                (half, half), [VMEM] * 3, (VMEM,) * 2, 2 * workers * block_bytes, flops,
            )(x_ready, ready[0], ready[1])
        )
    outs = ()
    shapes = (
        shape(workers, rows, wide), shape(rows, wide), shape(rows, stride), shape(rows, stride)
    )
    for j, (keep, send) in enumerate(halves):
        offset = j * width
        got = exchange(send, "worker", 1)
        blocks = call(
            add_kernel, (block,) * chips, [VMEM] * 2, (VMEM,) * chips,
            3 * chips * block_bytes,
        )(keep, got)
        parts = scatter_sum(blocks)
        delta = call(
            functools.partial(momentum_kernel, offset, stride, workers),
            block, [VMEM] * (len(parts) + 1), VMEM, (len(parts) + 2) * block_bytes,
        )(*parts, old)
        deltas = [delta]
        for q in range(1, regions):
            deltas.append(exchange(delta, "region", q))
        pulled, last, carried = call(
            functools.partial(merge_kernel, offset, regions),
            (block, shape(rows, width), shape(rows, width)),
            [VMEM] * (2 * regions + 1), (VMEM,) * 3, (regions + 4) * block_bytes,
        )(coef, *deltas, *states)
        pieces = gather_blocks(pulled, chips)
        early = [0, 1, 2, 4] if chips == 4 else list(range(workers // 2))
        late = [b for b in range(workers) if b not in early]
        for part, owners in (("a", early), ("b", late)):
            side = part == "a"
            given = [pieces[b] for b in owners] + ([delta, last, carried] if side else [])
            outs = call(
                functools.partial(place_kernel, offset, stride, owners, side, len(outs)),
                shapes,
                [VMEM] * len(given) + [HBM] * len(outs),
                (HBM,) * 4,
                2 * len(given) * block_bytes,
                scratch_shapes=[pltpu.SemaphoreType.DMA((regions * (len(owners) + 1) + 2,))],
                input_output_aliases={len(given) + i: i for i in range(len(outs))},
            )(*given, *outs)
    pulled, regional, params, momentum = outs
    return (regional[None], params, momentum, pulled.reshape(depth, wide)[None])


def solution(mesh):
    placed = (
        P("region", None, None),
        P("region", "worker", None, None, None),
        P(),
        P("region", "worker", None),
        P("worker", "region"),
        P("worker", "region"),
        P(),
        P(),
        P(),
    )

    return jax.shard_map(
        local,
        mesh=mesh,
        in_specs=placed,
        out_specs=(
            P("region", "worker", None),
            P("worker", "region"),
            P("worker", "region"),
            P("region", None, None),
        ),
        check_vma=False,
    )
```
